128 devices in a mesh: gr: 16 (over x, y), gc: 8 (over z, core).
Axes of the slice: x: 4, y: 4, z: 4, core: 2. Of those that a mesh axis runs over, the one named last changes fastest.
Arguments:
- child_rows: float32 [8192, 12288], P('gr', 'gc'), may hold values from -1.5 to 1.5
- row_map: int32 [8192], P('gr'), may hold values from 0 to 8191, as said below
- stair: int32 [64], replicated, may hold values from 0 to 896, as said below
Outputs:
- factor: float32 [1024, 12288], P('gr', 'gc')
- projected: float32 [8192, 12288], P('gr', 'gc')
The draws below stay inside these ranges and needn't reach their ends.
Inputs may be any that keep to these rules, and one draw needn't show every extreme that they name: row_map is a permutation of 0 to 8191. Of the 512 rows of one index of gr, at most 152 go to the rows of any one index of gr (row_map // 512), and some index of gr sends exactly 152 to one index. stair is nondecreasing and a multiple of 128; the first quarter of the blocks is 0 and the last block holds 896.
All inputs are finite; a program needn't handle non-finite values.
Results may differ from the reference program's by a relative error of at most 0.0003.
Values sent between devices are 32-bit elements; how exact they have to be, the bound alone decides.
A program may use at most 128 MiB of HBM per device.

```python
import jax
import jax.numpy as jnp
from jax import lax

NCOL = 12288
PANEL = 512
NPANEL = 2
STAIR_BLOCK = 128
ROWS_DEV = 512
ROWS = 8192
BLOCKS = 64
BASE = 24
N_GR = 16


def draw_row_map(key, part):
    key_pair, key_order, key_slot = jax.random.split(jax.random.fold_in(key, 11), 3)
    pairing = jax.random.permutation(key_pair, N_GR).astype(jnp.int32)
    heavy = ROWS_DEV - BASE * N_GR
    base_dest = jnp.repeat(jnp.arange(N_GR, dtype=jnp.int32), BASE)
    spread_part = jnp.broadcast_to(base_dest[None, :], (N_GR, BASE * N_GR))
    heavy_part = jnp.broadcast_to(pairing[:, None], (N_GR, heavy))
    targets = jnp.concatenate([spread_part, heavy_part], axis=1)
    iota_rows = jnp.arange(ROWS_DEV, dtype=jnp.int32)[None, :]
    scores = jax.random.randint(key_order, (N_GR, ROWS_DEV), 0, 1048576) * ROWS_DEV + iota_rows
    order = jnp.argsort(scores, axis=1)
    targets = jnp.take_along_axis(targets, order, axis=1)
    flat_dest = targets.reshape(-1)
    onehot = (flat_dest[:, None] == jnp.arange(N_GR, dtype=jnp.int32)[None, :]).astype(jnp.int32)
    rank_within = jnp.sum((jnp.cumsum(onehot, axis=0) - onehot) * onehot, axis=1)
    slot_scores = jax.random.randint(key_slot, (N_GR, ROWS_DEV), 0, 1048576) * ROWS_DEV + iota_rows
    slot_perm = jnp.argsort(slot_scores, axis=1).astype(jnp.int32)
    target_row = slot_perm[flat_dest, rank_within]
    return (flat_dest * ROWS_DEV + target_row).astype(jnp.int32)


def draw_stair(key, part):
    levels = 2 * PANEL // STAIR_BLOCK - 1
    values = jax.random.randint(jax.random.fold_in(key, 23), (BLOCKS,), 0, levels + 1)
    values = jnp.sort(values)
    block_ids = jnp.arange(BLOCKS, dtype=jnp.int32)
    values = jnp.where(block_ids < BLOCKS // 4, 0, values)
    values = jnp.where(block_ids == BLOCKS - 1, levels, values)
    return (values * STAIR_BLOCK).astype(jnp.int32)


def steps_of(own_key, shape, shards, smallest, largest):
    factor_of, own = 1.0, jax.random.fold_in(own_key, 6)
    for dim, shards_of in shards:
        draws = jnp.exp(jax.random.uniform(jax.random.fold_in(own, dim), (shards_of,), jnp.float32, smallest / len(shards), largest / len(shards)))
        factor_of = factor_of * jnp.repeat(draws, shape[dim] // shards_of).reshape([-1 if axis == dim else 1 for axis in range(len(shape))])
    return factor_of


def bell_draw(stream_key, dims, spread, most, cuts=(), held_as=jnp.bfloat16):
    values = jax.random.normal(stream_key, dims, jnp.float32) * spread
    if len(cuts) > 0:
        values = steps_of(stream_key, dims, cuts, -0.22, 0.18) * values
    return jnp.clip(values, min=-most, max=most).astype(held_as)


def setup_inputs(seed: int = 0) -> dict:
    key_list = jax.random.split(jax.random.key(seed), 4)
    child_rows = bell_draw(key_list[0], (ROWS, NCOL), 0.25, 1.5, ((0, 16), (1, 8)), jnp.float32)
    row_map = draw_row_map(jax.random.fold_in(key_list[3], 71), 0)
    stair = draw_stair(jax.random.fold_in(key_list[3], 71), 0)
    return dict(child_rows=child_rows, row_map=row_map, stair=stair)


def reference(child_rows, row_map, stair):
    front = jnp.zeros_like(child_rows).at[row_map].set(child_rows)
    row_ids = jnp.arange(front.shape[0], dtype=jnp.int32)
    col_ids = jnp.arange(front.shape[1], dtype=jnp.int32)
    limits = jnp.take(stair, row_ids // STAIR_BLOCK)
    front_work = jnp.where(col_ids[None, :] >= limits[:, None], front, jnp.zeros_like(front))
    blocks = []
    for step in range(NPANEL):
        panel_block = front_work[:, step * PANEL:(step + 1) * PANEL]
        basis_cols, triangle = jnp.linalg.qr(panel_block)
        signs = jnp.where(jnp.diagonal(triangle) < 0, -1.0, 1.0).astype(front_work.dtype)
        basis_cols = basis_cols * signs[None, :]
        coupling = jnp.dot(basis_cols.T.astype(jnp.float32), front_work.astype(jnp.float32), precision=lax.Precision.HIGHEST, preferred_element_type=jnp.float32)
        front_work = front_work - jnp.dot(basis_cols.astype(jnp.float32), coupling.astype(jnp.float32), precision=lax.Precision.HIGHEST, preferred_element_type=jnp.float32)
        blocks.append(coupling)
    return (jnp.concatenate(blocks, axis=0), front_work)
```

```python
import jax
import jax.numpy as jnp
from jax import lax
from jax.sharding import PartitionSpec as P

PANEL = 512
NPANEL = 2
STAIR_BLOCK = 128


def spread(value, axis, source):
    kept = jnp.where(lax.axis_index(axis) == source, value, 0).astype(value.dtype)
    return lax.psum(kept, axis)


def pack_rows(values, targets, groups):
    rows_dev = values.shape[0]
    base_rows = 3 * rows_dev // (4 * groups)
    capacity = rows_dev - base_rows * (groups - 1)
    target_dev = targets // rows_dev
    target_row = targets % rows_dev
    onehot = (target_dev[:, None] == jnp.arange(groups, dtype=jnp.int32)[None, :]).astype(jnp.int32)
    rank_within = jnp.sum((jnp.cumsum(onehot, axis=0) - onehot) * onehot, axis=1)
    buffer_index = target_dev * capacity + rank_within
    source_row = (
        jnp.full((groups * capacity,), rows_dev, jnp.int32)
        .at[buffer_index]
        .set(jnp.arange(rows_dev, dtype=jnp.int32))
    )
    sent_rows = jnp.take(values, source_row, axis=0, mode="fill", fill_value=0.0)
    sent_slots = (
        jnp.full((groups * capacity,), rows_dev, jnp.int32).at[buffer_index].set(target_row)
    )
    return (
        sent_rows.reshape(groups, capacity, values.shape[1]),
        sent_slots.reshape(groups, capacity),
    )


def place_rows(recv_rows, recv_slots, rows_dev):
    flat_rows = recv_rows.reshape(-1, recv_rows.shape[-1])
    flat_slots = recv_slots.reshape(-1)
    where_from = (
        jnp.zeros((rows_dev,), jnp.int32)
        .at[flat_slots]
        .set(jnp.arange(flat_slots.shape[0], dtype=jnp.int32), mode="drop")
    )
    return jnp.take(flat_rows, where_from, axis=0)


def matmul(left, right):
    return jnp.dot(left, right, precision=lax.Precision.HIGHEST, preferred_element_type=jnp.float32)


def high(left, right, contract):
    return lax.dot_general(
        left, right, (contract, ((), ())), precision=lax.Precision.HIGH,
        preferred_element_type=jnp.float32,
    )


def cholesky_inverse(gram):
    lower = jnp.linalg.cholesky(gram)
    eye = jnp.eye(gram.shape[0], dtype=gram.dtype)
    return jax.scipy.linalg.solve_triangular(lower, eye, lower=True)


def gram_inverse_factor(g00, g10, g11):
    i00 = cholesky_inverse(g00)
    l10 = matmul(g10, i00.T)
    i11 = cholesky_inverse(g11 - matmul(l10, l10.T))
    i10 = -matmul(i11, matmul(l10, i00))
    return jnp.concatenate(
        [jnp.concatenate([i00, jnp.zeros_like(i00)], 1), jnp.concatenate([i10, i11], 1)], 0
    )


def shards(child_rows, row_map, stair):
    groups = lax.axis_size("gr")
    rows_dev, cols_dev = child_rows.shape
    wide = NPANEL * PANEL
    half = PANEL // 2
    columns = lax.axis_index("gc") * cols_dev + jnp.arange(cols_dev, dtype=jnp.int32)
    limits = jnp.take(stair, row_map // STAIR_BLOCK)
    masked = jnp.where(columns[None, :] >= limits[:, None], child_rows, jnp.zeros_like(child_rows))

    own = masked[:, :wide]
    left = matmul(own.T, own[:, :PANEL])
    low = matmul(own[:, PANEL:].T, own[:, PANEL:])
    low = jnp.concatenate([low[:, :half], low[:, half:]], axis=0)
    gram = jnp.concatenate([left, low], axis=1)
    gram = jnp.where(lax.axis_index("gc") == 0, gram, jnp.zeros_like(gram))
    gram, masked, own = lax.optimization_barrier((gram, masked, own))
    gram = lax.psum(gram, ("gr", "gc"))

    sent_rows, sent_slots = pack_rows(masked, row_map, groups)
    recv_rows, recv_slots = (
        lax.all_to_all(sent_rows, "gr", split_axis=0, concat_axis=0, tiled=True),
        lax.all_to_all(sent_slots, "gr", split_axis=0, concat_axis=0, tiled=True),
    )
    own, gram = lax.optimization_barrier((own, gram))
    panel = spread(own, "gc", 0)
    local = high(panel, masked, ((0,), (0,)))
    products = lax.psum(local, "gr")

    low = jnp.concatenate([gram[:PANEL, PANEL:], gram[PANEL:, PANEL:]], axis=1)
    inverse = gram_inverse_factor(gram[:PANEL, :PANEL], gram[PANEL:, :PANEL], low)

    front = place_rows(recv_rows, recv_slots, rows_dev)
    front_own, _ = lax.optimization_barrier((front[:, :wide], local))
    front_panel = spread(front_own, "gc", 0)
    basis = high(front_panel, inverse, ((1,), (1,)))
    stacked = high(inverse, products, ((1,), (0,)))
    projected = front - high(basis, stacked, ((1,), (0,)))
    share_rows = wide // groups
    factor = lax.dynamic_slice_in_dim(stacked, lax.axis_index("gr") * share_rows, share_rows, 0)
    return (factor, projected)


def solution(mesh):
    placed = (P("gr", "gc"), P("gr"), P())
    return jax.shard_map(
        shards,
        mesh=mesh,
        in_specs=placed,
        out_specs=(P("gr", "gc"), P("gr", "gc")),
        check_vma=False,
    )
```

```python
import jax
import jax.numpy as jnp
from jax import lax
from jax.sharding import PartitionSpec as P

PANEL = 512
NPANEL = 2
STAIR_BLOCK = 128


def spread(value, axis, source):
    kept = jnp.where(lax.axis_index(axis) == source, value, 0).astype(value.dtype)
    return lax.psum(kept, axis)


def pack_rows(values, targets, groups):
    rows_dev = values.shape[0]
    base_rows = 3 * rows_dev // (4 * groups)
    capacity = rows_dev - base_rows * (groups - 1)
    target_dev = targets // rows_dev
    target_row = targets % rows_dev
    onehot = (target_dev[:, None] == jnp.arange(groups, dtype=jnp.int32)[None, :]).astype(jnp.int32)
    rank_within = jnp.sum((jnp.cumsum(onehot, axis=0) - onehot) * onehot, axis=1)
    buffer_index = target_dev * capacity + rank_within
    source_row = (
        jnp.full((groups * capacity,), rows_dev, jnp.int32)
        .at[buffer_index]
        .set(jnp.arange(rows_dev, dtype=jnp.int32))
    )
    sent_rows = jnp.take(values, source_row, axis=0, mode="fill", fill_value=0.0)
    sent_slots = (
        jnp.full((groups * capacity,), rows_dev, jnp.int32).at[buffer_index].set(target_row)
    )
    return (
        sent_rows.reshape(groups, capacity, values.shape[1]),
        sent_slots.reshape(groups, capacity),
    )


def place_rows(recv_rows, recv_slots, rows_dev):
    flat_rows = recv_rows.reshape(-1, recv_rows.shape[-1])
    flat_slots = recv_slots.reshape(-1)
    where_from = (
        jnp.zeros((rows_dev,), jnp.int32)
        .at[flat_slots]
        .set(jnp.arange(flat_slots.shape[0], dtype=jnp.int32), mode="drop")
    )
    return jnp.take(flat_rows, where_from, axis=0)


def matmul(left, right):
    return jnp.dot(left, right, precision=lax.Precision.HIGHEST, preferred_element_type=jnp.float32)


def high(left, right, contract):
    return lax.dot_general(
        left, right, (contract, ((), ())), precision=lax.Precision.HIGH,
        preferred_element_type=jnp.float32,
    )


def inverse_factor(upper, size):
    count = upper.shape[0] // size
    eye = jnp.eye(size, dtype=upper.dtype)
    done = jnp.zeros((upper.shape[0], 0), upper.dtype)
    rest = upper
    rows = []
    for k in range(count):
        lower = lax.linalg.cholesky(rest[:size, :size], symmetrize_input=False)
        small = lax.linalg.triangular_solve(lower, eye, left_side=True, lower=True)
        scaled = matmul(small, jnp.concatenate([rest[:size, size:], done[:size]], axis=1))
        right = rest.shape[1] - size
        rows.append(
            jnp.concatenate(
                [scaled[:, right:], small, jnp.zeros((size, right), upper.dtype)], axis=1
            )
        )
        if right > 0:
            terms = jnp.concatenate([scaled, small], axis=1)
            taken = lax.dot_general(
                scaled[:, :right], terms, (((0,), (0,)), ((), ())),
                precision=lax.Precision.HIGHEST, preferred_element_type=jnp.float32,
            )
            rest = rest[size:, size:] - taken[:, :right]
            fresh = jnp.zeros((right, size), upper.dtype)
            done = jnp.concatenate([done[size:], fresh], axis=1) - taken[:, right:]
    return jnp.concatenate(rows, axis=0)


def shards(child_rows, row_map, stair):
    groups = lax.axis_size("gr")
    rows_dev, cols_dev = child_rows.shape
    wide = NPANEL * PANEL
    half = PANEL // 2
    columns = lax.axis_index("gc") * cols_dev + jnp.arange(cols_dev, dtype=jnp.int32)
    limits = jnp.take(stair, row_map // STAIR_BLOCK)
    masked = jnp.where(columns[None, :] >= limits[:, None], child_rows, jnp.zeros_like(child_rows))

    sent_rows, sent_slots = pack_rows(masked, row_map, groups)
    recv_slots = lax.all_to_all(sent_slots, "gr", split_axis=0, concat_axis=0, tiled=True)

    panel = spread(masked[:, :wide], "gc", 0)
    first, second = panel[:, :PANEL], panel[:, PANEL:]
    local = high(panel, masked, ((0,), (0,)))
    top = matmul(first.T, panel)
    low = matmul(second.T, second)
    left = jnp.concatenate([top[:, :PANEL], top[:, PANEL:]], axis=0)
    low = jnp.concatenate([low[:, :half], low[:, half:]], axis=0)
    sums = lax.psum(jnp.concatenate([local, left, low], axis=1), "gr")

    sums, sent_rows = lax.optimization_barrier((sums, sent_rows))
    recv_rows = lax.all_to_all(sent_rows, "gr", split_axis=0, concat_axis=0, tiled=True)
    products = sums[:, :cols_dev]
    gram = sums[:, cols_dev:]
    low = jnp.concatenate([gram[:PANEL, PANEL:], gram[PANEL:, PANEL:]], axis=1)
    top = jnp.concatenate([gram[:PANEL, :PANEL], gram[PANEL:, :PANEL]], axis=1)
    low = jnp.concatenate([jnp.zeros_like(low), low], axis=1)
    inverse = inverse_factor(jnp.concatenate([top, low], axis=0), STAIR_BLOCK)

    front = place_rows(recv_rows, recv_slots, rows_dev)
    front_panel = spread(front[:, :wide], "gc", 0)
    basis = high(front_panel, inverse, ((1,), (1,)))
    stacked = high(inverse, products, ((1,), (0,)))
    projected = front - high(basis, stacked, ((1,), (0,)))
    share_rows = wide // groups
    factor = lax.dynamic_slice_in_dim(stacked, lax.axis_index("gr") * share_rows, share_rows, 0)
    return (factor, projected)


def solution(mesh):
    placed = (P("gr", "gc"), P("gr"), P())
    return jax.shard_map(
        shards,
        mesh=mesh,
        in_specs=placed,
        out_specs=(P("gr", "gc"), P("gr", "gc")),
        check_vma=False,
    )
```
